32 devices in a mesh: group: 2 (over y), pix: 16 (over z, x, core).
Axes of the slice: x: 2, y: 2, z: 4, core: 2. Of those that a mesh axis runs over, the one named last changes fastest.
Arguments:
- images: bfloat16 [256, 2, 120, 840], P(('group', 'pix')), parts along dimension 0, may hold values from -170 to 170
- valid_mask: int32 [256, 840], P(('group', 'pix')), parts along dimension 0, may hold values from 0 to 1
Outputs:
- look_coherence: bfloat16 [128, 40, 2, 120, 120], P(('group', 'pix')), parts along dimension 0
- slab_coherence: float32 [4, 120, 120], P('group'), parts along dimension 0
The draws below stay inside these ranges and needn't reach their ends.
There are 2 independent parts, one for each index of `group`. The reference program is written for one: setup_inputs(seed, part) draws one part's arguments, and reference() takes and returns one part's arrays. A program takes and returns all parts, laid end to end along the dimension named above; each array names one. Nothing has to cross between parts.
All inputs are finite; a program needn't handle non-finite values.
Results may differ from the reference program's by a relative error of at most 0.001.
Values may be sent and summed in bfloat16 or wider, within the bound.
A program may use at most 128 MiB of HBM per device.

```python
import math
import jax
import jax.numpy as jnp
from jax import lax

M = 120
ROWS = 128
COLS = 840


def draw_images(key, part):
    keys = jax.random.split(key, 6)
    signal = jnp.clip(jax.random.normal(keys[0], (ROWS, 2, 1, COLS), jnp.float32), -3.5, 3.5)
    noise = jnp.clip(jax.random.normal(keys[1], (ROWS, 2, M, COLS), jnp.float32), -5.0, 5.0)
    common = 2.0
    rate_block = jnp.exp(jax.random.uniform(keys[2], (ROWS // 4, COLS // 21), jnp.float32, math.log(0.005), math.log(0.2)))
    rates = jnp.repeat(jnp.repeat(rate_block, 4, axis=0), 21, axis=1)
    acq_index = jnp.arange(M, dtype=jnp.float32)
    weights = common * jnp.exp(-rates[:, None, :] * acq_index[None, :, None])
    phase_block = jax.random.uniform(keys[5], (ROWS // 4, M), jnp.float32, -math.pi, math.pi)
    phases = jnp.repeat(phase_block, 4, axis=0)
    cosine = jnp.cos(phases)[:, :, None]
    sine = jnp.sin(phases)[:, :, None]
    sig_re = signal[:, 0]
    sig_im = signal[:, 1]
    rot_re = weights * (sig_re * cosine - sig_im * sine)
    rot_im = weights * (sig_re * sine + sig_im * cosine)
    rotated = jnp.stack([rot_re, rot_im], axis=1)
    acq_scale = jnp.exp(jax.random.uniform(keys[3], (M,), jnp.float32, math.log(0.5), math.log(2.0)))
    rough = jnp.exp(jax.random.uniform(keys[4], (ROWS, COLS), jnp.float32, math.log(0.7), math.log(1.4)))
    pixel_scale = rough
    values = (rotated + noise) * acq_scale[None, None, :, None] * pixel_scale[:, None, None, :]
    return values.astype(jnp.bfloat16)


def draw_valid_mask(key, part):
    keys = jax.random.split(key, 3)
    first = jax.random.randint(keys[0], (ROWS, COLS), 0, 12)
    second = jax.random.randint(keys[1], (ROWS, COLS), 0, 12)
    level_draw = jax.random.randint(keys[2], (ROWS // 4, COLS // 21), 0, 24)
    levels = jnp.where(level_draw == 0, 0, jnp.where(level_draw == 1, 3, 11 + level_draw % 2))
    levels = jnp.repeat(jnp.repeat(levels, 4, axis=0), 21, axis=1)
    band = 11 + 2 * jnp.arange(ROWS, dtype=jnp.int32) // ROWS
    valid = (first < levels) & (second < band[:, None])
    return valid.astype(jnp.int32)


def setup_inputs(seed: int = 0, part: int = 0) -> dict:
    key_list = jax.random.split(jax.random.key(seed), 3)
    own_keys = jax.random.split(jax.random.fold_in(key_list[2], part), 3)
    images = draw_images(jax.random.fold_in(jax.random.fold_in(key_list[2], part), 71), part)
    valid_mask = draw_valid_mask(jax.random.fold_in(jax.random.fold_in(key_list[2], part), 71), part)
    return {"images": images, "valid_mask": valid_mask}


floor_power = 30.0

def split_parts(grams):
    real_part = grams[..., 0, :, 0, :] + grams[..., 1, :, 1, :]
    imag_part = grams[..., 1, :, 0, :] - grams[..., 0, :, 1, :]
    return (real_part, imag_part)

def coherence(real_part, imag_part, with_floor):
    powers = jnp.diagonal(real_part, axis1=-2, axis2=-1)
    if with_floor:
        powers = jnp.maximum(powers, floor_power)
    scaled = jnp.sqrt(powers[..., :, None] * powers[..., None, :])
    return jnp.stack([real_part / scaled, imag_part / scaled], axis=-3)

def reference(images, valid_mask):
    masked = images * valid_mask[:, None, None, :].astype(jnp.bfloat16)
    widened = masked.astype(jnp.float32)
    slab_grams = jnp.einsum('rkic,rhjc->kihj', widened, widened)
    slab_real, slab_imag = split_parts(slab_grams)
    slab_coherence = coherence(slab_real, slab_imag, False)
    padded = jnp.pad(widened, ((3, 3), (0, 0), (0, 0), (0, 0)))
    acq_count = images.shape[2]
    look_cols = images.shape[3] // 21

    def one_look(look_index):
        window_data = lax.dynamic_slice_in_dim(padded, (2 * look_index).astype(jnp.int32), 7, 0)
        blocks = window_data.reshape(7, 2, acq_count, look_cols, 21)
        grams = jnp.einsum('rkilq,rhjlq->lkihj', blocks, blocks)
        real_part, imag_part = split_parts(grams)
        return coherence(real_part, imag_part, True).astype(jnp.bfloat16)
    look_coherence = lax.map(one_look, jnp.arange(ROWS // 2, dtype=jnp.int32))
    return (look_coherence, slab_coherence)
```

```python
import functools

import jax
import jax.numpy as jnp
from jax import lax
from jax.experimental import pallas as pl
from jax.experimental.pallas import tpu as pltpu
from jax.sharding import PartitionSpec as P

floor_power = 30.0
look_width = 21
lane = 128
below = 3
above = 2
per_group = 5
MESH = pl.DeviceIdType.MESH
NT = (((1,), (1,)), ((), ()))


def group_start(g, cols):
    return min(g * per_group * look_width, cols - lane)


def looks_kernel(rows, acq, cols, low_ref, own_ref, high_ref, valid_ref, out_ref, z, v, lhs, acc):
    g = pl.program_id(0)
    groups = cols // (look_width * per_group)
    total = rows + below + above
    width = 2 * lane

    def put(r, image, weights):
        a, b = image[0], image[1]
        even = pl.ds(pl.multiple_of(r * width, lane), lane)
        odd = pl.ds(pl.multiple_of(r * width + lane, lane), lane)
        for n in range(groups):
            s = group_start(n, cols)
            pa, pb = a[:, s : s + lane], b[:, s : s + lane]
            z[n, 0:acq, even] = pa
            z[n, 0:acq, odd] = pb
            z[n, lane : lane + acq, even] = -pb
            z[n, lane : lane + acq, odd] = pa
            w = jnp.ones((1, lane), jnp.float32) if weights is None else weights[:, s : s + lane]
            v[n, :, even] = w
            v[n, :, odd] = w

    @pl.when(g == 0)
    def _():
        @pl.loop(0, groups)
        def _(n):
            zeros = jnp.zeros((lane - acq, z.shape[2]), jnp.bfloat16)
            z[n, acq:lane, :] = zeros
            z[n, lane + acq : 2 * lane, :] = zeros

        @pl.loop(0, below)
        def _(r):
            put(r, low_ref[r], None)

        @pl.loop(0, rows)
        def _(r):
            put(r + below, own_ref[r], valid_ref[r])

        @pl.loop(0, above)
        def _(r):
            put(r + below + rows, high_ref[r], None)

    first = g * per_group * look_width
    offset = first - jnp.minimum(first, cols - lane)
    lanes = jnp.bitwise_and(lax.broadcasted_iota(jnp.int32, (1, total * width), 1), lane - 1)
    weights = v[g]
    for n in range(per_group):
        lo = offset + n * look_width
        inside = (lanes >= lo) & (lanes < lo + look_width)
        chosen = jnp.where(inside, weights, 0.0).astype(jnp.bfloat16)
        lhs[n * lane : (n + 1) * lane, :] = z[g, 0:lane, :] * chosen

    def gram(first_row, last_row):
        k = pl.ds(first_row * width, (last_row - first_row + 1) * width)
        return lax.dot_general(lhs[:, k], z[g, :, k], NT, preferred_element_type=jnp.float32)

    row_index = lax.broadcasted_iota(jnp.int32, (lane, lane), 0)
    col_index = lax.broadcasted_iota(jnp.int32, (lane, lane), 1)
    eye = row_index == col_index

    def finish(look, slot):
        @pl.loop(0, per_group)
        def _(n):
            at = pl.ds(pl.multiple_of(n * lane, lane), lane)
            real = acc[slot, at, 0:lane]
            imag = acc[slot, at, lane:width]
            diag = jnp.where(eye, real, 0.0)
            down = lax.rsqrt(jnp.maximum(jnp.sum(diag, axis=1, keepdims=True), floor_power))
            across = lax.rsqrt(jnp.maximum(jnp.sum(diag, axis=0, keepdims=True), floor_power))
            real = real * down * across
            imag = imag * down * across
            out_ref[look, n, 0] = real[0:acq, 0:acq].astype(jnp.bfloat16)
            out_ref[look, n, 1] = imag[0:acq, 0:acq].astype(jnp.bfloat16)

    for pair in range(rows // 4):
        r = 4 * pair
        common = gram(r + 2, r + 6)
        acc[0] = common + gram(r, r + 1)
        acc[1] = common + gram(r + 7, r + 8)
        finish(2 * pair, 0)
        finish(2 * pair + 1, 1)


def look_coherences(low, own, high, valid):
    rows, _, acq, cols = own.shape
    look_cols = cols // look_width
    groups = look_cols // per_group
    total = rows + below + above
    full = lambda shape: pl.BlockSpec(
        shape, lambda g: (0,) * len(shape), pipeline_mode=pl.Buffered(1)
    )
    return pl.pallas_call(
        functools.partial(looks_kernel, rows, acq, cols),
        grid=(groups,),
        out_shape=jax.ShapeDtypeStruct((rows // 2, look_cols, 2, acq, acq), jnp.bfloat16),
        in_specs=[full(low.shape), full(own.shape), full(high.shape), full(valid.shape)],
        out_specs=pl.BlockSpec((rows // 2, per_group, 2, acq, acq), lambda g: (0, g, 0, 0, 0)),
        scratch_shapes=[
            pltpu.VMEM((groups, 2 * lane, total * 2 * lane), jnp.bfloat16),
            pltpu.VMEM((groups, 1, total * 2 * lane), jnp.float32),
            pltpu.VMEM((per_group * lane, total * 2 * lane), jnp.bfloat16),
            pltpu.VMEM((2, per_group * lane, 2 * lane), jnp.float32),
        ],
        compiler_params=pltpu.CompilerParams(vmem_limit_bytes=56 << 20),
        cost_estimate=pl.CostEstimate(
            flops=18 * 10**9, bytes_accessed=16 * 10**6, transcendentals=0
        ),
        name="looks",
    )(low, own, high, valid)


def slab_kernel(rows, acq, cols, own_ref, valid_ref, packed_ref, z, acc):
    z[...] = jnp.zeros_like(z)
    acc[...] = jnp.zeros_like(acc)

    @pl.loop(0, rows)
    def _(r):
        image = own_ref[r]
        z[0:acq, :] = image[0]
        z[lane : lane + acq, :] = image[1]
        full = z[...]
        left = full * valid_ref[r].astype(jnp.bfloat16)
        acc[...] += lax.dot_general(left, full, NT, preferred_element_type=jnp.float32)

    real = acc[0:lane, 0:lane] + acc[lane:, lane:]
    imag = acc[lane:, 0:lane] - acc[0:lane, lane:]
    row_index = lax.broadcasted_iota(jnp.int32, (lane, lane), 0)
    col_index = lax.broadcasted_iota(jnp.int32, (lane, lane), 1)
    packed = jnp.where(row_index >= col_index, real, imag)
    for n in range(packed_ref.shape[0]):
        packed_ref[n] = packed[8 * n : 8 * n + 8, :]


def slab_gram(own, valid):
    rows, _, acq, cols = own.shape
    return pl.pallas_call(
        functools.partial(slab_kernel, rows, acq, cols),
        out_shape=jax.ShapeDtypeStruct((pl.cdiv(acq, 8), 8, lane), jnp.float32),
        in_specs=[pl.BlockSpec(memory_space=pltpu.VMEM)] * 2,
        out_specs=pl.BlockSpec(memory_space=pltpu.VMEM),
        scratch_shapes=[
            pltpu.VMEM((2 * lane, cols), jnp.bfloat16),
            pltpu.VMEM((2 * lane, 2 * lane), jnp.float32),
        ],
        compiler_params=pltpu.CompilerParams(vmem_limit_bytes=32 << 20),
        cost_estimate=pl.CostEstimate(
            flops=10**9, bytes_accessed=4 * 10**6, transcendentals=0
        ),
        name="slab",
    )(own, valid)


def reduce_kernel(
    count, acq, packed_ref, out_ref, inbox, mine, result, send1, recv1, send2, recv2
):
    me = lax.axis_index("pix")
    owners = packed_ref.shape[0]

    barrier = pltpu.get_barrier_semaphore()

    @pl.loop(1, count)
    def _(o):
        peer = lax.rem(me + o, count)
        pl.semaphore_signal(barrier, inc=1, device_id={"pix": peer}, device_id_type=MESH)

    pl.semaphore_wait(barrier, count - 1)

    def scatter(peer):
        return pltpu.make_async_remote_copy(
            src_ref=packed_ref.at[peer],
            dst_ref=inbox.at[me],
            send_sem=send1.at[peer],
            recv_sem=recv1.at[me],
            device_id={"pix": peer},
            device_id_type=MESH,
        )

    def arrived(peer):
        return pltpu.make_async_remote_copy(
            src_ref=packed_ref.at[0],
            dst_ref=inbox.at[peer],
            send_sem=send1.at[0],
            recv_sem=recv1.at[peer],
            device_id={"pix": peer},
            device_id_type=MESH,
        )

    def spread(peer):
        return pltpu.make_async_remote_copy(
            src_ref=mine,
            dst_ref=result.at[me],
            send_sem=send2.at[peer],
            recv_sem=recv2.at[me],
            device_id={"pix": peer},
            device_id_type=MESH,
        )

    def gathered(peer):
        return pltpu.make_async_remote_copy(
            src_ref=mine,
            dst_ref=result.at[peer],
            send_sem=send2.at[peer],
            recv_sem=recv2.at[peer],
            device_id={"pix": peer},
            device_id_type=MESH,
        )

    @pl.loop(1, count)
    def _(o):
        peer = lax.rem(me + o, count)

        @pl.when(peer < owners)
        def _():
            scatter(peer).start()

    @pl.when(me < owners)
    def _():
        inbox[me] = packed_ref[me]

        @pl.loop(1, count)
        def _(o):
            arrived(lax.rem(me + o, count)).wait_recv()

        mine[...] = jnp.sum(inbox[...], axis=0)
        result[me] = mine[...]

        @pl.loop(1, count)
        def _(o):
            spread(lax.rem(me + o, count)).start()

    @pl.loop(1, count)
    def _(o):
        peer = lax.rem(me + o, count)

        @pl.when(peer < owners)
        def _():
            gathered(peer).wait_recv()

    packed = jnp.concatenate(
        [result[n] for n in range(owners)] + [jnp.zeros((lane - 8 * owners, lane), jnp.float32)],
        axis=0,
    )
    flipped = packed.T
    row_index = lax.broadcasted_iota(jnp.int32, (lane, lane), 0)
    col_index = lax.broadcasted_iota(jnp.int32, (lane, lane), 1)
    real = jnp.where(row_index >= col_index, packed, flipped)
    imag = jnp.where(row_index < col_index, packed, -flipped)
    imag = jnp.where(row_index == col_index, 0.0, imag)
    diag = jnp.where(row_index == col_index, packed, 0.0)
    scale = jnp.sqrt(jnp.sum(diag, axis=1, keepdims=True) * jnp.sum(diag, axis=0, keepdims=True))
    out_ref[0] = (real / scale)[0:acq, 0:acq]
    out_ref[1] = (imag / scale)[0:acq, 0:acq]

    @pl.loop(1, count)
    def _(o):
        peer = lax.rem(me + o, count)

        @pl.when(peer < owners)
        def _():
            scatter(peer).wait_send()

        @pl.when(me < owners)
        def _():
            spread(peer).wait_send()


def slab_reduce(packed, count, acq):
    owners = packed.shape[0]
    return pl.pallas_call(
        functools.partial(reduce_kernel, count, acq),
        out_shape=jax.ShapeDtypeStruct((2, acq, acq), jnp.float32),
        in_specs=[pl.BlockSpec(memory_space=pltpu.VMEM)],
        out_specs=pl.BlockSpec(memory_space=pltpu.VMEM),
        scratch_shapes=[
            pltpu.VMEM((count, 8, lane), jnp.float32),
            pltpu.VMEM((8, lane), jnp.float32),
            pltpu.VMEM((owners, 8, lane), jnp.float32),
            pltpu.SemaphoreType.DMA((owners,)),
            pltpu.SemaphoreType.DMA((count,)),
            pltpu.SemaphoreType.DMA((count,)),
            pltpu.SemaphoreType.DMA((count,)),
        ],
        compiler_params=pltpu.CompilerParams(collective_id=0, has_side_effects=True),
        name="slab_reduce",
    )(packed)


def shards(count, images, valid_mask):
    rows, _, acq, cols = images.shape
    valid = valid_mask.astype(jnp.float32)[:, None, :]
    keep = valid_mask[:, None, None, :].astype(jnp.bfloat16)
    forward = [(i, i + 1) for i in range(count - 1)]
    backward = [(i + 1, i) for i in range(count - 1)]
    low = lax.ppermute(images[rows - below :] * keep[rows - below :], "pix", forward)
    high = lax.ppermute(images[:above] * keep[:above], "pix", backward)
    packed = slab_gram(images, valid)
    slab = slab_reduce(packed, count, acq)
    looks = look_coherences(low, images, high, valid)
    return looks, slab


def solution(mesh):
    count = mesh.shape["pix"]
    in_specs = (P(("group", "pix"), None, None, None), P(("group", "pix"), None))
    out_specs = (P(("group", "pix"), None, None, None, None), P("group", None, None))
    return jax.shard_map(
        functools.partial(shards, count),
        mesh=mesh,
        in_specs=in_specs,
        out_specs=out_specs,
        check_vma=False,
    )
```

```python
import functools

import jax
import jax.numpy as jnp
from jax import lax
from jax.experimental import pallas as pl
from jax.experimental.pallas import tpu as pltpu
from jax.sharding import PartitionSpec as P

floor_power = 30.0
look_width = 21
lane = 128
below = 3
above = 2
per_group = 5
MESH = pl.DeviceIdType.MESH
NT = (((1,), (1,)), ((), ()))


def group_start(g, cols):
    return min(g * per_group * look_width, cols - lane)


def looks_kernel(rows, acq, cols, low_ref, own_ref, high_ref, valid_ref, out_ref, z, v, lhs, acc):
    g = pl.program_id(0)
    groups = cols // (look_width * per_group)
    total = rows + below + above
    width = 2 * lane

    def put(r, image, weights):
        a, b = image[0], image[1]
        even = pl.ds(pl.multiple_of(r * width, lane), lane)
        odd = pl.ds(pl.multiple_of(r * width + lane, lane), lane)
        for n in range(groups):
            s = group_start(n, cols)
            pa, pb = a[:, s : s + lane], b[:, s : s + lane]
            z[n, 0:acq, even] = pa
            z[n, 0:acq, odd] = pb
            z[n, lane : lane + acq, even] = -pb
            z[n, lane : lane + acq, odd] = pa
            w = jnp.ones((1, lane), jnp.float32) if weights is None else weights[:, s : s + lane]
            v[n, :, even] = w
            v[n, :, odd] = w

    @pl.when(g == 0)
    def _():
        @pl.loop(0, groups)
        def _(n):
            zeros = jnp.zeros((lane - acq, z.shape[2]), jnp.bfloat16)
            z[n, acq:lane, :] = zeros
            z[n, lane + acq : 2 * lane, :] = zeros

        @pl.loop(0, below)
        def _(r):
            put(r, low_ref[r], None)

        @pl.loop(0, rows)
        def _(r):
            put(r + below, own_ref[r], valid_ref[r])

        @pl.loop(0, above)
        def _(r):
            put(r + below + rows, high_ref[r], None)

    first = g * per_group * look_width
    offset = first - jnp.minimum(first, cols - lane)
    lanes = jnp.bitwise_and(lax.broadcasted_iota(jnp.int32, (1, total * width), 1), lane - 1)
    weights = v[g]
    for n in range(per_group):
        lo = offset + n * look_width
        inside = (lanes >= lo) & (lanes < lo + look_width)
        chosen = jnp.where(inside, weights, 0.0).astype(jnp.bfloat16)
        lhs[n * lane : (n + 1) * lane, :] = z[g, 0:lane, :] * chosen

    def gram(first_row, last_row):
        k = pl.ds(first_row * width, (last_row - first_row + 1) * width)
        return lax.dot_general(lhs[:, k], z[g, :, k], NT, preferred_element_type=jnp.float32)

    row_index = lax.broadcasted_iota(jnp.int32, (lane, lane), 0)
    col_index = lax.broadcasted_iota(jnp.int32, (lane, lane), 1)
    eye = row_index == col_index

    def finish(look, slot):
        for n in range(per_group):
            at = pl.ds(n * lane, lane)
            real = acc[slot, at, 0:lane]
            imag = acc[slot, at, lane:width]
            diag = jnp.where(eye, real, 0.0)
            down = lax.rsqrt(jnp.maximum(jnp.sum(diag, axis=1, keepdims=True), floor_power))
            across = lax.rsqrt(jnp.maximum(jnp.sum(diag, axis=0, keepdims=True), floor_power))
            real = real * down * across
            imag = imag * down * across
            out_ref[look, n, 0] = real[0:acq, 0:acq].astype(jnp.bfloat16)
            out_ref[look, n, 1] = imag[0:acq, 0:acq].astype(jnp.bfloat16)

    for pair in range(rows // 4):
        r = 4 * pair
        common = gram(r + 2, r + 6)
        acc[0] = common + gram(r, r + 1)
        acc[1] = common + gram(r + 7, r + 8)
        finish(2 * pair, 0)
        finish(2 * pair + 1, 1)


def look_coherences(low, own, high, valid):
    rows, _, acq, cols = own.shape
    look_cols = cols // look_width
    groups = look_cols // per_group
    total = rows + below + above
    full = lambda shape: pl.BlockSpec(
        shape, lambda g: (0,) * len(shape), pipeline_mode=pl.Buffered(1)
    )
    return pl.pallas_call(
        functools.partial(looks_kernel, rows, acq, cols),
        grid=(groups,),
        out_shape=jax.ShapeDtypeStruct((rows // 2, look_cols, 2, acq, acq), jnp.bfloat16),
        in_specs=[full(low.shape), full(own.shape), full(high.shape), full(valid.shape)],
        out_specs=pl.BlockSpec((rows // 2, per_group, 2, acq, acq), lambda g: (0, g, 0, 0, 0)),
        scratch_shapes=[
            pltpu.VMEM((groups, 2 * lane, total * 2 * lane), jnp.bfloat16),
            pltpu.VMEM((groups, 1, total * 2 * lane), jnp.float32),
            pltpu.VMEM((per_group * lane, total * 2 * lane), jnp.bfloat16),
            pltpu.VMEM((2, per_group * lane, 2 * lane), jnp.float32),
        ],
        compiler_params=pltpu.CompilerParams(vmem_limit_bytes=56 << 20),
        cost_estimate=pl.CostEstimate(
            flops=18 * 10**9, bytes_accessed=16 * 10**6, transcendentals=0
        ),
        name="looks",
    )(low, own, high, valid)


def slab_kernel(rows, acq, cols, own_ref, valid_ref, packed_ref, z, acc):
    z[...] = jnp.zeros_like(z)
    acc[...] = jnp.zeros_like(acc)

    @pl.loop(0, rows)
    def _(r):
        image = own_ref[r]
        z[0:acq, :] = image[0]
        z[lane : lane + acq, :] = image[1]
        full = z[...]
        left = full * valid_ref[r].astype(jnp.bfloat16)
        acc[...] += lax.dot_general(left, full, NT, preferred_element_type=jnp.float32)

    real = acc[0:lane, 0:lane] + acc[lane:, lane:]
    imag = acc[lane:, 0:lane] - acc[0:lane, lane:]
    row_index = lax.broadcasted_iota(jnp.int32, (lane, lane), 0)
    col_index = lax.broadcasted_iota(jnp.int32, (lane, lane), 1)
    packed = jnp.where(row_index >= col_index, real, imag)
    for n in range(packed_ref.shape[0]):
        packed_ref[n] = packed[8 * n : 8 * n + 8, :]


def slab_gram(own, valid):
    rows, _, acq, cols = own.shape
    return pl.pallas_call(
        functools.partial(slab_kernel, rows, acq, cols),
        out_shape=jax.ShapeDtypeStruct((pl.cdiv(acq, 8), 8, lane), jnp.float32),
        in_specs=[pl.BlockSpec(memory_space=pltpu.VMEM)] * 2,
        out_specs=pl.BlockSpec(memory_space=pltpu.VMEM),
        scratch_shapes=[
            pltpu.VMEM((2 * lane, cols), jnp.bfloat16),
            pltpu.VMEM((2 * lane, 2 * lane), jnp.float32),
        ],
        compiler_params=pltpu.CompilerParams(vmem_limit_bytes=32 << 20),
        cost_estimate=pl.CostEstimate(
            flops=10**9, bytes_accessed=4 * 10**6, transcendentals=0
        ),
        name="slab",
    )(own, valid)


def reduce_kernel(
    count, acq, packed_ref, out_ref, inbox, mine, result, send1, recv1, send2, recv2
):
    me = lax.axis_index("pix")
    owners = packed_ref.shape[0]

    barrier = pltpu.get_barrier_semaphore()

    @pl.loop(1, count)
    def _(o):
        peer = lax.rem(me + o, count)
        pl.semaphore_signal(barrier, inc=1, device_id={"pix": peer}, device_id_type=MESH)

    pl.semaphore_wait(barrier, count - 1)

    def scatter(peer):
        return pltpu.make_async_remote_copy(
            src_ref=packed_ref.at[peer],
            dst_ref=inbox.at[me],
            send_sem=send1.at[peer],
            recv_sem=recv1.at[me],
            device_id={"pix": peer},
            device_id_type=MESH,
        )

    def arrived(peer):
        return pltpu.make_async_remote_copy(
            src_ref=packed_ref.at[0],
            dst_ref=inbox.at[peer],
            send_sem=send1.at[0],
            recv_sem=recv1.at[peer],
            device_id={"pix": peer},
            device_id_type=MESH,
        )

    def spread(peer):
        return pltpu.make_async_remote_copy(
            src_ref=mine,
            dst_ref=result.at[me],
            send_sem=send2.at[peer],
            recv_sem=recv2.at[me],
            device_id={"pix": peer},
            device_id_type=MESH,
        )

    def gathered(peer):
        return pltpu.make_async_remote_copy(
            src_ref=mine,
            dst_ref=result.at[peer],
            send_sem=send2.at[peer],
            recv_sem=recv2.at[peer],
            device_id={"pix": peer},
            device_id_type=MESH,
        )

    @pl.loop(1, count)
    def _(o):
        peer = lax.rem(me + o, count)

        @pl.when(peer < owners)
        def _():
            scatter(peer).start()

    @pl.when(me < owners)
    def _():
        inbox[me] = packed_ref[me]

        @pl.loop(1, count)
        def _(o):
            arrived(lax.rem(me + o, count)).wait_recv()

        mine[...] = jnp.sum(inbox[...], axis=0)
        result[me] = mine[...]

        @pl.loop(1, count)
        def _(o):
            spread(lax.rem(me + o, count)).start()

    @pl.loop(1, count)
    def _(o):
        peer = lax.rem(me + o, count)

        @pl.when(peer < owners)
        def _():
            gathered(peer).wait_recv()

    packed = jnp.concatenate(
        [result[n] for n in range(owners)] + [jnp.zeros((lane - 8 * owners, lane), jnp.float32)],
        axis=0,
    )
    flipped = packed.T
    row_index = lax.broadcasted_iota(jnp.int32, (lane, lane), 0)
    col_index = lax.broadcasted_iota(jnp.int32, (lane, lane), 1)
    real = jnp.where(row_index >= col_index, packed, flipped)
    imag = jnp.where(row_index < col_index, packed, -flipped)
    imag = jnp.where(row_index == col_index, 0.0, imag)
    diag = jnp.where(row_index == col_index, packed, 0.0)
    scale = jnp.sqrt(jnp.sum(diag, axis=1, keepdims=True) * jnp.sum(diag, axis=0, keepdims=True))
    out_ref[0] = (real / scale)[0:acq, 0:acq]
    out_ref[1] = (imag / scale)[0:acq, 0:acq]

    @pl.loop(1, count)
    def _(o):
        peer = lax.rem(me + o, count)

        @pl.when(peer < owners)
        def _():
            scatter(peer).wait_send()

        @pl.when(me < owners)
        def _():
            spread(peer).wait_send()


def slab_reduce(packed, count, acq):
    owners = packed.shape[0]
    return pl.pallas_call(
        functools.partial(reduce_kernel, count, acq),
        out_shape=jax.ShapeDtypeStruct((2, acq, acq), jnp.float32),
        in_specs=[pl.BlockSpec(memory_space=pltpu.VMEM)],
        out_specs=pl.BlockSpec(memory_space=pltpu.VMEM),
        scratch_shapes=[
            pltpu.VMEM((count, 8, lane), jnp.float32),
            pltpu.VMEM((8, lane), jnp.float32),
            pltpu.VMEM((owners, 8, lane), jnp.float32),
            pltpu.SemaphoreType.DMA((owners,)),
            pltpu.SemaphoreType.DMA((count,)),
            pltpu.SemaphoreType.DMA((count,)),
            pltpu.SemaphoreType.DMA((count,)),
        ],
        compiler_params=pltpu.CompilerParams(collective_id=0, has_side_effects=True),
        name="slab_reduce",
    )(packed)


def shards(count, images, valid_mask):
    rows, _, acq, cols = images.shape
    valid = valid_mask.astype(jnp.float32)[:, None, :]
    keep = valid_mask[:, None, None, :].astype(jnp.bfloat16)
    forward = [(i, i + 1) for i in range(count - 1)]
    backward = [(i + 1, i) for i in range(count - 1)]
    low = lax.ppermute(images[rows - below :] * keep[rows - below :], "pix", forward)
    high = lax.ppermute(images[:above] * keep[:above], "pix", backward)
    packed = slab_gram(images, valid)
    slab = slab_reduce(packed, count, acq)
    looks = look_coherences(low, images, high, valid)
    return looks, slab


def solution(mesh):
    count = mesh.shape["pix"]
    in_specs = (P(("group", "pix"), None, None, None), P(("group", "pix"), None))
    out_specs = (P(("group", "pix"), None, None, None, None), P("group", None, None))
    return jax.shard_map(
        functools.partial(shards, count),
        mesh=mesh,
        in_specs=in_specs,
        out_specs=out_specs,
        check_vma=False,
    )
```

```python
import functools

import jax
import jax.numpy as jnp
from jax import lax
from jax.experimental import pallas as pl
from jax.experimental.pallas import tpu as pltpu
from jax.sharding import PartitionSpec as P

floor_power = 30.0
look_width = 21
lane = 128
below = 3
above = 2
width = 2 * lane
per_group = 5
MESH = pl.DeviceIdType.MESH
NT = (((1,), (1,)), ((), ()))


def group_start(g, cols):
    return min(g * per_group * look_width, cols - lane)


def put(z, v, acq, cols, r, image, weights):
    a, b = image[0], image[1]
    even = pl.ds(pl.multiple_of(r * width, lane), lane)
    odd = pl.ds(pl.multiple_of(r * width + lane, lane), lane)
    for n in range(z.shape[0]):
        s = group_start(n, cols)
        pa, pb = a[:, s : s + lane], b[:, s : s + lane]
        z[n, 0:acq, even] = pa
        z[n, 0:acq, odd] = pb
        z[n, lane : lane + acq, even] = -pb
        z[n, lane : lane + acq, odd] = pa
        w = weights[:, s : s + lane]
        v[n, :, even] = w
        v[n, :, odd] = w


def clear_padding(z, acq):
    @pl.loop(0, z.shape[0])
    def _(n):
        zeros = jnp.zeros((lane - acq, z.shape[2]), jnp.bfloat16)
        z[n, acq:lane, :] = zeros
        z[n, lane + acq : 2 * lane, :] = zeros


def masked_looks(lhs, x, weights, g, cols):
    first = g * per_group * look_width
    offset = first - jnp.minimum(first, cols - lane)
    lanes = jnp.bitwise_and(lax.broadcasted_iota(jnp.int32, weights.shape, 1), lane - 1)
    for n in range(per_group):
        lo = offset + n * look_width
        inside = (lanes >= lo) & (lanes < lo + look_width)
        chosen = jnp.where(inside, weights, 0.0).astype(jnp.bfloat16)
        lhs[n * lane : (n + 1) * lane, :] = x * chosen


def gram(lhs, first_row, last_row, right):
    k = pl.ds(first_row * width, (last_row - first_row + 1) * width)
    return lax.dot_general(lhs[:, k], right[:, k], NT, preferred_element_type=jnp.float32)


def finish(acc, acq, store):
    row_index = lax.broadcasted_iota(jnp.int32, (lane, lane), 0)
    col_index = lax.broadcasted_iota(jnp.int32, (lane, lane), 1)
    eye = row_index == col_index
    for n in range(per_group):
        at = pl.ds(n * lane, lane)
        real = acc[at, 0:lane]
        imag = acc[at, lane:width]
        diag = jnp.where(eye, real, 0.0)
        down = lax.rsqrt(jnp.maximum(jnp.sum(diag, axis=1, keepdims=True), floor_power))
        across = lax.rsqrt(jnp.maximum(jnp.sum(diag, axis=0, keepdims=True), floor_power))
        real = real * down * across
        imag = imag * down * across
        store(n, 0, real[0:acq, 0:acq].astype(jnp.bfloat16))
        store(n, 1, imag[0:acq, 0:acq].astype(jnp.bfloat16))


def exchange_kernel(
    count, rows, acq, cols,
    own_ref, valid_ref,
    low_ref, high_ref, vlow_ref, vhigh_ref, z_hbm, inner_hbm, slab_ref,
    z, v, lhs, acc, inner, packed_ref, inbox, mine, result, full, gram_acc, zeros,
    halo_send, halo_recv, z_sem, inner_sem, zero_sem, send1, recv1, send2, recv2,
):
    me = lax.axis_index("pix")
    owners = packed_ref.shape[0]
    groups = z.shape[0]
    barrier = pltpu.get_barrier_semaphore()

    @pl.loop(1, count)
    def _(o):
        peer = lax.rem(me + o, count)
        pl.semaphore_signal(barrier, inc=1, device_id={"pix": peer}, device_id_type=MESH)

    pl.semaphore_wait(barrier, count - 1)

    def halo(n):
        right = n % 2 == 0
        size = below if right else above
        src, dst = ((own_ref, (low_ref, high_ref)), (valid_ref, (vlow_ref, vhigh_ref)))[n // 2]
        start = rows - size if right else 0
        return pltpu.make_async_remote_copy(
            src_ref=src.at[pl.ds(start, size)],
            dst_ref=dst[0 if right else 1],
            send_sem=halo_send.at[n],
            recv_sem=halo_recv.at[n],
            device_id={"pix": me + 1 if right else me - 1},
            device_id_type=MESH,
        )

    @pl.when(me < count - 1)
    def _():
        halo(0).start()
        halo(2).start()

    @pl.when(me > 0)
    def _():
        halo(1).start()
        halo(3).start()

    def blank(dst, vdst, size):
        image = pltpu.make_async_copy(zeros.at[pl.ds(0, size)], dst, zero_sem)
        image.start()
        image.wait()
        vdst[...] = jnp.zeros_like(vdst)

    @pl.when(me == 0)
    def _():
        zeros[...] = jnp.zeros_like(zeros)
        blank(low_ref, vlow_ref, below)

    @pl.when(me == count - 1)
    def _():
        zeros[...] = jnp.zeros_like(zeros)
        blank(high_ref, vhigh_ref, above)

    full[...] = jnp.zeros_like(full)
    gram_acc[...] = jnp.zeros_like(gram_acc)

    @pl.loop(0, rows)
    def _(r):
        image = own_ref[r]
        full[0:acq, :] = image[0]
        full[lane : lane + acq, :] = image[1]
        both = full[...]
        left = both * valid_ref[r].astype(jnp.bfloat16)
        gram_acc[...] += lax.dot_general(left, both, NT, preferred_element_type=jnp.float32)

    real = gram_acc[0:lane, 0:lane] + gram_acc[lane:, lane:]
    imag = gram_acc[lane:, 0:lane] - gram_acc[0:lane, lane:]
    row_index = lax.broadcasted_iota(jnp.int32, (lane, lane), 0)
    col_index = lax.broadcasted_iota(jnp.int32, (lane, lane), 1)
    packed = jnp.where(row_index >= col_index, real, imag)
    for n in range(owners):
        packed_ref[n] = packed[8 * n : 8 * n + 8, :]

    def remote(src, dst, send, recv, peer):
        return pltpu.make_async_remote_copy(
            src_ref=src, dst_ref=dst, send_sem=send, recv_sem=recv,
            device_id={"pix": peer}, device_id_type=MESH,
        )

    def scatter(peer):
        return remote(packed_ref.at[peer], inbox.at[me], send1.at[peer], recv1.at[me], peer)

    def arrived(peer):
        return remote(packed_ref.at[0], inbox.at[peer], send1.at[0], recv1.at[peer], peer)

    def spread(peer):
        return remote(mine, result.at[me], send2.at[peer], recv2.at[me], peer)

    def gathered(peer):
        return remote(mine, result.at[peer], send2.at[peer], recv2.at[peer], peer)

    @pl.loop(1, count)
    def _(o):
        peer = lax.rem(me + o, count)

        @pl.when(peer < owners)
        def _():
            scatter(peer).start()

    clear_padding(z, acq)

    @pl.loop(0, rows)
    def _(r):
        put(z, v, acq, cols, r, own_ref[r], valid_ref[r])

    z_copy = pltpu.make_async_copy(z, z_hbm, z_sem)
    z_copy.start()

    def inner_copy(g):
        at = pl.ds(g * per_group, per_group)
        return pltpu.make_async_copy(inner.at[at], inner_hbm.at[at], inner_sem.at[g])

    def inner_group(g):
        masked_looks(lhs, z[g, 0:lane, :], v[g], g, cols)
        acc[...] = gram(lhs, 1, rows - 1, z.at[g])

        def store(n, part, value):
            inner[g * per_group + n, part] = value

        finish(acc, acq, store)
        inner_copy(g).start()

    @pl.loop(0, groups - 1)
    def _(g):
        inner_group(g)

    @pl.when(me < owners)
    def _():
        inbox[me] = packed_ref[me]

        @pl.loop(1, count)
        def _(o):
            arrived(lax.rem(me + o, count)).wait_recv()

        mine[...] = jnp.sum(inbox[...], axis=0)
        result[me] = mine[...]

        @pl.loop(1, count)
        def _(o):
            spread(lax.rem(me + o, count)).start()

    inner_group(groups - 1)

    @pl.loop(1, count)
    def _(o):
        peer = lax.rem(me + o, count)

        @pl.when(peer < owners)
        def _():
            gathered(peer).wait_recv()

    packed = jnp.concatenate(
        [result[n] for n in range(owners)] + [jnp.zeros((lane - 8 * owners, lane), jnp.float32)],
        axis=0,
    )
    flipped = packed.T
    real = jnp.where(row_index >= col_index, packed, flipped)
    imag = jnp.where(row_index < col_index, packed, -flipped)
    imag = jnp.where(row_index == col_index, 0.0, imag)
    diag = jnp.where(row_index == col_index, packed, 0.0)
    scale = jnp.sqrt(jnp.sum(diag, axis=1, keepdims=True) * jnp.sum(diag, axis=0, keepdims=True))
    slab_ref[0] = (real / scale)[0:acq, 0:acq]
    slab_ref[1] = (imag / scale)[0:acq, 0:acq]

    z_copy.wait()

    @pl.loop(0, groups)
    def _(g):
        inner_copy(g).wait()

    @pl.loop(1, count)
    def _(o):
        peer = lax.rem(me + o, count)

        @pl.when(peer < owners)
        def _():
            scatter(peer).wait_send()

        @pl.when(me < owners)
        def _():
            spread(peer).wait_send()

    @pl.when(me < count - 1)
    def _():
        halo(0).wait_send()
        halo(2).wait_send()
        halo(1).wait_recv()
        halo(3).wait_recv()

    @pl.when(me > 0)
    def _():
        halo(1).wait_send()
        halo(3).wait_send()
        halo(0).wait_recv()
        halo(2).wait_recv()


def exchange(count, own, valid):
    rows, _, acq, cols = own.shape
    look_cols = cols // look_width
    groups = look_cols // per_group
    owners = pl.cdiv(acq, 8)
    vmem = pl.BlockSpec(memory_space=pltpu.VMEM)
    hbm = pl.BlockSpec(memory_space=pl.ANY)
    bf16, f32 = jnp.bfloat16, jnp.float32
    dma = pltpu.SemaphoreType.DMA
    return pl.pallas_call(
        functools.partial(exchange_kernel, count, rows, acq, cols),
        out_shape=(
            jax.ShapeDtypeStruct((below, 2, acq, cols), bf16),
            jax.ShapeDtypeStruct((above, 2, acq, cols), bf16),
            jax.ShapeDtypeStruct((below, 1, cols), f32),
            jax.ShapeDtypeStruct((above, 1, cols), f32),
            jax.ShapeDtypeStruct((groups, 2 * lane, rows * width), bf16),
            jax.ShapeDtypeStruct((look_cols, 2, acq, acq), bf16),
            jax.ShapeDtypeStruct((2, acq, acq), f32),
        ),
        in_specs=[vmem, vmem],
        out_specs=(hbm, hbm, vmem, vmem, hbm, hbm, vmem),
        scratch_shapes=[
            pltpu.VMEM((groups, 2 * lane, rows * width), bf16),
            pltpu.VMEM((groups, 1, rows * width), f32),
            pltpu.VMEM((per_group * lane, rows * width), bf16),
            pltpu.VMEM((per_group * lane, width), f32),
            pltpu.VMEM((look_cols, 2, acq, acq), bf16),
            pltpu.VMEM((owners, 8, lane), f32),
            pltpu.VMEM((count, 8, lane), f32),
            pltpu.VMEM((8, lane), f32),
            pltpu.VMEM((owners, 8, lane), f32),
            pltpu.VMEM((2 * lane, cols), bf16),
            pltpu.VMEM((2 * lane, 2 * lane), f32),
            pltpu.VMEM((below, 2, acq, cols), bf16),
            dma((4,)), dma((4,)), dma, dma((groups,)), dma,
            dma((owners,)), dma((count,)), dma((count,)), dma((count,)),
        ],
        compiler_params=pltpu.CompilerParams(
            collective_id=0, has_side_effects=True, vmem_limit_bytes=48 << 20
        ),
        name="exchange",
    )(own, valid)


def looks_kernel(
    rows, acq, cols,
    z_ref, inner_ref, valid_ref, low_ref, vlow_ref, high_ref, vhigh_ref,
    out_ref, z, v, v_own, lhs, lhs_halo, acc0, acc1, acc3,
):
    g = pl.program_id(0)
    halo = below + above

    @pl.when(g == 0)
    def _():
        clear_padding(z, acq)

        @pl.loop(0, below)
        def _(r):
            put(z, v, acq, cols, r, low_ref[r], vlow_ref[r])

        @pl.loop(0, above)
        def _(r):
            put(z, v, acq, cols, r + below, high_ref[r], vhigh_ref[r])

        for r in range(rows):
            for n in range(v_own.shape[0]):
                s = group_start(n, cols)
                w = valid_ref[r][:, s : s + lane]
                v_own[n, :, pl.ds(r * width, lane)] = w
                v_own[n, :, pl.ds(r * width + lane, lane)] = w

    own, edge = z_ref.at[0], z.at[g]
    masked_looks(lhs, z_ref[0, 0:lane, :], v_own[g], g, cols)
    masked_looks(lhs_halo, z[g, 0:lane, :], v[g], g, cols)

    def store(look):
        def put_out(n, part, value):
            out_ref[look, n, part] = value
        return put_out

    half = rows // 2
    common = gram(lhs, 0, half - 1, own)
    acc0[...] = common + gram(lhs_halo, 0, below - 1, edge)
    acc1[...] = common + (gram(lhs, half, half + 1, own) + gram(lhs_halo, below - 1, below - 1, edge))
    finish(acc0, acq, store(0))
    acc3[...] = gram(lhs, rows - 5, rows - 1, own) + gram(lhs_halo, below, halo - 1, edge)
    finish(acc1, acq, store(1))
    out_ref[2] = inner_ref[...]
    finish(acc3, acq, store(3))


def look_coherences(z, inner, valid, low, vlow, high, vhigh):
    groups, _, wide = z.shape
    rows = wide // width
    look_cols, _, acq, _ = inner.shape
    cols = valid.shape[-1]
    whole = [valid, low, vlow, high, vhigh]
    full = lambda shape: pl.BlockSpec(
        shape, lambda g: (0,) * len(shape), pipeline_mode=pl.Buffered(1)
    )
    return pl.pallas_call(
        functools.partial(looks_kernel, rows, acq, cols),
        grid=(groups,),
        out_shape=jax.ShapeDtypeStruct((rows // 2, look_cols, 2, acq, acq), jnp.bfloat16),
        in_specs=[
            pl.BlockSpec((1, 2 * lane, wide), lambda g: (g, 0, 0)),
            pl.BlockSpec((per_group, 2, acq, acq), lambda g: (g, 0, 0, 0)),
        ] + [full(x.shape) for x in whole],
        out_specs=pl.BlockSpec((rows // 2, per_group, 2, acq, acq), lambda g: (0, g, 0, 0, 0)),
        scratch_shapes=[
            pltpu.VMEM((groups, 2 * lane, (below + above) * width), jnp.bfloat16),
            pltpu.VMEM((groups, 1, (below + above) * width), jnp.float32),
            pltpu.VMEM((groups, 1, wide), jnp.float32),
            pltpu.VMEM((per_group * lane, wide), jnp.bfloat16),
            pltpu.VMEM((per_group * lane, (below + above) * width), jnp.bfloat16),
        ] + [pltpu.VMEM((per_group * lane, width), jnp.float32)] * 3,
        compiler_params=pltpu.CompilerParams(vmem_limit_bytes=48 << 20),
        name="looks",
    )(z, inner, *whole)


def shards(count, images, valid_mask):
    valid = valid_mask.astype(jnp.float32)[:, None, :]
    low, high, vlow, vhigh, z, inner, slab = exchange(count, images, valid)
    looks = look_coherences(z, inner, valid, low, vlow, high, vhigh)
    return looks, slab


def solution(mesh):
    count = mesh.shape["pix"]
    in_specs = (P(("group", "pix"), None, None, None), P(("group", "pix"), None))
    out_specs = (P(("group", "pix"), None, None, None, None), P("group", None, None))
    return jax.shard_map(
        functools.partial(shards, count),
        mesh=mesh,
        in_specs=in_specs,
        out_specs=out_specs,
        check_vma=False,
    )
```

```python
import functools

import jax
import jax.numpy as jnp
from jax import lax
from jax.experimental import pallas as pl
from jax.experimental.pallas import tpu as pltpu
from jax.sharding import PartitionSpec as P

floor_power = 30.0
look_width = 21
lane = 128
below = 3
above = 2
width = 2 * lane
per_group = 5
MESH = pl.DeviceIdType.MESH
NT = (((1,), (1,)), ((), ()))


def group_start(g, cols):
    return min(g * per_group * look_width, cols - lane)


def put(z, v, acq, cols, r, image, weights):
    a, b = image[0], image[1]
    even = pl.ds(pl.multiple_of(r * width, lane), lane)
    odd = pl.ds(pl.multiple_of(r * width + lane, lane), lane)
    for n in range(z.shape[0]):
        s = group_start(n, cols)
        pa, pb = a[:, s : s + lane], b[:, s : s + lane]
        z[n, 0:acq, even] = pa
        z[n, 0:acq, odd] = pb
        z[n, lane : lane + acq, even] = -pb
        z[n, lane : lane + acq, odd] = pa
        w = weights[:, s : s + lane]
        v[n, :, even] = w
        v[n, :, odd] = w


def clear_padding(z, acq):
    @pl.loop(0, z.shape[0])
    def _(n):
        zeros = jnp.zeros((lane - acq, z.shape[2]), jnp.bfloat16)
        z[n, acq:lane, :] = zeros
        z[n, lane + acq : 2 * lane, :] = zeros


def masked_looks(lhs, x, weights, g, cols):
    first = g * per_group * look_width
    offset = first - jnp.minimum(first, cols - lane)
    lanes = jnp.bitwise_and(lax.broadcasted_iota(jnp.int32, weights.shape, 1), lane - 1)
    for n in range(per_group):
        lo = offset + n * look_width
        inside = (lanes >= lo) & (lanes < lo + look_width)
        chosen = jnp.where(inside, weights, 0.0).astype(jnp.bfloat16)
        lhs[n * lane : (n + 1) * lane, :] = x * chosen


def gram(lhs, first_row, last_row, right):
    k = pl.ds(first_row * width, (last_row - first_row + 1) * width)
    return lax.dot_general(lhs[:, k], right[:, k], NT, preferred_element_type=jnp.float32)


def finish(acc, acq, store):
    row_index = lax.broadcasted_iota(jnp.int32, (lane, lane), 0)
    col_index = lax.broadcasted_iota(jnp.int32, (lane, lane), 1)
    eye = row_index == col_index
    for n in range(per_group):
        at = pl.ds(n * lane, lane)
        real = acc[at, 0:lane]
        imag = acc[at, lane:width]
        diag = jnp.where(eye, real, 0.0)
        down = lax.rsqrt(jnp.maximum(jnp.sum(diag, axis=1, keepdims=True), floor_power))
        across = lax.rsqrt(jnp.maximum(jnp.sum(diag, axis=0, keepdims=True), floor_power))
        real = real * down * across
        imag = imag * down * across
        store(n, 0, real[0:acq, 0:acq].astype(jnp.bfloat16))
        store(n, 1, imag[0:acq, 0:acq].astype(jnp.bfloat16))


def exchange_kernel(
    count, rows, acq, cols,
    own_ref, valid_ref,
    low_ref, vlow_ref, z_hbm, inner_hbm, slab_ref,
    high_ref, vhigh_ref, z_high, v_high, lhs_high, acc_high,
    z, v, lhs, acc, inner, packed_ref, inbox, mine, result, full, gram_acc, zeros,
    halo_send, halo_recv, z_sem, inner_sem, zero_sem, send1, recv1, send2, recv2,
):
    me = lax.axis_index("pix")
    owners = packed_ref.shape[0]
    groups = z.shape[0]
    barrier = pltpu.get_barrier_semaphore()

    @pl.loop(1, count)
    def _(o):
        peer = lax.rem(me + o, count)
        pl.semaphore_signal(barrier, inc=1, device_id={"pix": peer}, device_id_type=MESH)

    pl.semaphore_wait(barrier, count - 1)

    def to_right(n):
        return halo(n, me + 1)

    def to_left(n):
        return halo(below + 1 + n, me - 1)

    def halo(n, peer):
        if n <= below:
            src, dst = (own_ref, low_ref) if n < below else (valid_ref, vlow_ref)
            at = pl.ds(rows - 1 - n, 1) if n < below else pl.ds(rows - below, below)
            to = pl.ds(below - 1 - n, 1) if n < below else pl.ds(0, below)
        else:
            m = n - below - 1
            src, dst = (own_ref, high_ref) if m < above else (valid_ref, vhigh_ref)
            at = to = pl.ds(m, 1) if m < above else pl.ds(0, above)
        return pltpu.make_async_remote_copy(
            src_ref=src.at[at], dst_ref=dst.at[to],
            send_sem=halo_send.at[n], recv_sem=halo_recv.at[n],
            device_id={"pix": peer}, device_id_type=MESH,
        )

    rights = (below,) + tuple(range(below))
    lefts = (above,) + tuple(range(above))

    def send(to_the_right, to_the_left):
        @pl.when(me < count - 1)
        def _():
            for n in to_the_right:
                to_right(n).start()

        @pl.when(me > 0)
        def _():
            for n in to_the_left:
                to_left(n).start()

    send(rights[:2], lefts[:2])

    def blank(dst, vdst, size):
        image = pltpu.make_async_copy(zeros.at[pl.ds(0, size)], dst, zero_sem)
        image.start()
        image.wait()
        vdst[...] = jnp.zeros_like(vdst)

    @pl.when(me == 0)
    def _():
        zeros[...] = jnp.zeros_like(zeros)
        blank(low_ref, vlow_ref, below)

    @pl.when(me == count - 1)
    def _():
        high_ref[...] = jnp.zeros_like(high_ref)
        vhigh_ref[...] = jnp.zeros_like(vhigh_ref)

    full[...] = jnp.zeros_like(full)
    gram_acc[...] = jnp.zeros_like(gram_acc)

    @pl.loop(0, rows)
    def _(r):
        image = own_ref[r]
        full[0:acq, :] = image[0]
        full[lane : lane + acq, :] = image[1]
        both = full[...]
        left = both * valid_ref[r].astype(jnp.bfloat16)
        gram_acc[...] += lax.dot_general(left, both, NT, preferred_element_type=jnp.float32)

    real = gram_acc[0:lane, 0:lane] + gram_acc[lane:, lane:]
    imag = gram_acc[lane:, 0:lane] - gram_acc[0:lane, lane:]
    row_index = lax.broadcasted_iota(jnp.int32, (lane, lane), 0)
    col_index = lax.broadcasted_iota(jnp.int32, (lane, lane), 1)
    packed = jnp.where(row_index >= col_index, real, imag)
    for n in range(owners):
        packed_ref[n] = packed[8 * n : 8 * n + 8, :]

    def remote(src, dst, send, recv, peer):
        return pltpu.make_async_remote_copy(
            src_ref=src, dst_ref=dst, send_sem=send, recv_sem=recv,
            device_id={"pix": peer}, device_id_type=MESH,
        )

    def scatter(peer):
        return remote(packed_ref.at[peer], inbox.at[me], send1.at[peer], recv1.at[me], peer)

    def arrived(peer):
        return remote(packed_ref.at[0], inbox.at[peer], send1.at[0], recv1.at[peer], peer)

    def spread(peer):
        return remote(mine, result.at[me], send2.at[peer], recv2.at[me], peer)

    def gathered(peer):
        return remote(mine, result.at[peer], send2.at[peer], recv2.at[peer], peer)

    @pl.loop(1, count)
    def _(o):
        peer = lax.rem(me + o, count)

        @pl.when(peer < owners)
        def _():
            scatter(peer).start()

    send(rights[2:3], lefts[2:])

    clear_padding(z, acq)

    @pl.loop(0, rows)
    def _(r):
        put(z, v, acq, cols, r, own_ref[r], valid_ref[r])

    z_copy = pltpu.make_async_copy(z, z_hbm, z_sem)
    z_copy.start()

    def inner_copy(look, g):
        at = pl.ds(g * per_group, per_group)
        return pltpu.make_async_copy(inner.at[look, at], inner_hbm.at[look, at], inner_sem.at[look, g])

    def inner_group(g):
        masked_looks(lhs, z[g, 0:lane, :], v[g], g, cols)
        acc[...] = gram(lhs, 1, rows - 1, z.at[g])

        def store(n, part, value):
            inner[0, g * per_group + n, part] = value

        finish(acc, acq, store)
        inner_copy(0, g).start()

    @pl.when(me < owners)
    def _():
        inbox[me] = packed_ref[me]

        @pl.loop(1, count)
        def _(o):
            arrived(lax.rem(me + o, count)).wait_recv()

        mine[...] = jnp.sum(inbox[...], axis=0)
        result[me] = mine[...]

        @pl.loop(1, count)
        def _(o):
            spread(lax.rem(me + o, count)).start()

    send(rights[3:], ())

    @pl.loop(0, groups)
    def _(g):
        inner_group(g)

    @pl.loop(1, count)
    def _(o):
        peer = lax.rem(me + o, count)

        @pl.when(peer < owners)
        def _():
            gathered(peer).wait_recv()

    packed = jnp.concatenate(
        [result[n] for n in range(owners)] + [jnp.zeros((lane - 8 * owners, lane), jnp.float32)],
        axis=0,
    )
    flipped = packed.T
    real = jnp.where(row_index >= col_index, packed, flipped)
    imag = jnp.where(row_index < col_index, packed, -flipped)
    imag = jnp.where(row_index == col_index, 0.0, imag)
    diag = jnp.where(row_index == col_index, packed, 0.0)
    scale = jnp.sqrt(jnp.sum(diag, axis=1, keepdims=True) * jnp.sum(diag, axis=0, keepdims=True))
    slab_ref[0] = (real / scale)[0:acq, 0:acq]
    slab_ref[1] = (imag / scale)[0:acq, 0:acq]

    @pl.when(me < count - 1)
    def _():
        for n in lefts:
            to_left(n).wait_recv()

    clear_padding(z_high, acq)

    @pl.loop(0, above)
    def _(r):
        put(z_high, v_high, acq, cols, r, high_ref[r], vhigh_ref[r])

    @pl.loop(0, groups)
    def _(g):
        masked_looks(lhs, z[g, 0:lane, :], v[g], g, cols)
        masked_looks(lhs_high, z_high[g, 0:lane, :], v_high[g], g, cols)
        acc_high[...] = gram(lhs, rows - 5, rows - 1, z.at[g]) + gram(
            lhs_high, 0, above - 1, z_high.at[g]
        )

        def store(n, part, value):
            inner[1, g * per_group + n, part] = value

        finish(acc_high, acq, store)
        inner_copy(1, g).start()

    z_copy.wait()

    @pl.loop(0, groups)
    def _(g):
        inner_copy(0, g).wait()
        inner_copy(1, g).wait()

    @pl.loop(1, count)
    def _(o):
        peer = lax.rem(me + o, count)

        @pl.when(peer < owners)
        def _():
            scatter(peer).wait_send()

        @pl.when(me < owners)
        def _():
            spread(peer).wait_send()

    @pl.when(me < count - 1)
    def _():
        for n in rights:
            to_right(n).wait_send()

    @pl.when(me > 0)
    def _():
        for n in lefts:
            to_left(n).wait_send()
        for n in rights:
            to_right(n).wait_recv()


def exchange(count, own, valid):
    rows, _, acq, cols = own.shape
    look_cols = cols // look_width
    groups = look_cols // per_group
    owners = pl.cdiv(acq, 8)
    vmem = pl.BlockSpec(memory_space=pltpu.VMEM)
    hbm = pl.BlockSpec(memory_space=pl.ANY)
    bf16, f32 = jnp.bfloat16, jnp.float32
    dma = pltpu.SemaphoreType.DMA
    return pl.pallas_call(
        functools.partial(exchange_kernel, count, rows, acq, cols),
        out_shape=(
            jax.ShapeDtypeStruct((below, 2, acq, cols), bf16),
            jax.ShapeDtypeStruct((below, 1, cols), f32),
            jax.ShapeDtypeStruct((groups, 2 * lane, rows * width), bf16),
            jax.ShapeDtypeStruct((2, look_cols, 2, acq, acq), bf16),
            jax.ShapeDtypeStruct((2, acq, acq), f32),
        ),
        in_specs=[vmem, vmem],
        out_specs=(hbm, vmem, hbm, hbm, vmem),
        scratch_shapes=[
            pltpu.VMEM((above, 2, acq, cols), bf16),
            pltpu.VMEM((above, 1, cols), f32),
            pltpu.VMEM((groups, 2 * lane, above * width), bf16),
            pltpu.VMEM((groups, 1, above * width), f32),
            pltpu.VMEM((per_group * lane, above * width), bf16),
            pltpu.VMEM((per_group * lane, width), f32),
            pltpu.VMEM((groups, 2 * lane, rows * width), bf16),
            pltpu.VMEM((groups, 1, rows * width), f32),
            pltpu.VMEM((per_group * lane, rows * width), bf16),
            pltpu.VMEM((per_group * lane, width), f32),
            pltpu.VMEM((2, look_cols, 2, acq, acq), bf16),
            pltpu.VMEM((owners, 8, lane), f32),
            pltpu.VMEM((count, 8, lane), f32),
            pltpu.VMEM((8, lane), f32),
            pltpu.VMEM((owners, 8, lane), f32),
            pltpu.VMEM((2 * lane, cols), bf16),
            pltpu.VMEM((2 * lane, 2 * lane), f32),
            pltpu.VMEM((below, 2, acq, cols), bf16),
            dma((below + above + 2,)), dma((below + above + 2,)), dma, dma((2, groups)), dma,
            dma((owners,)), dma((count,)), dma((count,)), dma((count,)),
        ],
        compiler_params=pltpu.CompilerParams(
            collective_id=0, has_side_effects=True, vmem_limit_bytes=48 << 20
        ),
        name="exchange",
    )(own, valid)


def looks_kernel(
    rows, acq, cols,
    z_ref, inner_ref, valid_ref, low_ref, vlow_ref,
    out_ref, z, v, v_own, lhs, lhs_halo, acc0, acc1,
):
    g = pl.program_id(0)
    @pl.when(g == 0)
    def _():
        clear_padding(z, acq)

        @pl.loop(0, below)
        def _(r):
            put(z, v, acq, cols, r, low_ref[r], vlow_ref[r])

        for r in range(rows):
            for n in range(v_own.shape[0]):
                s = group_start(n, cols)
                w = valid_ref[r][:, s : s + lane]
                v_own[n, :, pl.ds(r * width, lane)] = w
                v_own[n, :, pl.ds(r * width + lane, lane)] = w

    own, edge = z_ref.at[0], z.at[g]
    used = (rows // 2 + 2) * width
    masked_looks(lhs, z_ref[0, 0:lane, 0:used], v_own[g, :, 0:used], g, cols)
    masked_looks(lhs_halo, z[g, 0:lane, :], v[g], g, cols)

    def store(look):
        def put_out(n, part, value):
            out_ref[look, n, part] = value
        return put_out

    half = rows // 2
    common = gram(lhs, 0, half - 1, own)
    acc0[...] = common + gram(lhs_halo, 0, below - 1, edge)
    acc1[...] = common + (gram(lhs, half, half + 1, own) + gram(lhs_halo, below - 1, below - 1, edge))
    finish(acc0, acq, store(0))
    finish(acc1, acq, store(1))
    out_ref[2:4] = inner_ref[...]


def look_coherences(z, inner, valid, low, vlow):
    groups, _, wide = z.shape
    rows = wide // width
    _, look_cols, _, acq, _ = inner.shape
    cols = valid.shape[-1]
    whole = [valid, low, vlow]
    full = lambda shape: pl.BlockSpec(
        shape, lambda g: (0,) * len(shape), pipeline_mode=pl.Buffered(1)
    )
    return pl.pallas_call(
        functools.partial(looks_kernel, rows, acq, cols),
        grid=(groups,),
        out_shape=jax.ShapeDtypeStruct((rows // 2, look_cols, 2, acq, acq), jnp.bfloat16),
        in_specs=[
            pl.BlockSpec((1, 2 * lane, wide), lambda g: (g, 0, 0)),
            pl.BlockSpec((2, per_group, 2, acq, acq), lambda g: (0, g, 0, 0, 0)),
        ] + [full(x.shape) for x in whole],
        out_specs=pl.BlockSpec((rows // 2, per_group, 2, acq, acq), lambda g: (0, g, 0, 0, 0)),
        scratch_shapes=[
            pltpu.VMEM((groups, 2 * lane, below * width), jnp.bfloat16),
            pltpu.VMEM((groups, 1, below * width), jnp.float32),
            pltpu.VMEM((groups, 1, wide), jnp.float32),
            pltpu.VMEM((per_group * lane, (rows // 2 + 2) * width), jnp.bfloat16),
            pltpu.VMEM((per_group * lane, below * width), jnp.bfloat16),
        ] + [pltpu.VMEM((per_group * lane, width), jnp.float32)] * 2,
        compiler_params=pltpu.CompilerParams(vmem_limit_bytes=48 << 20),
        name="looks",
    )(z, inner, *whole)


def shards(count, images, valid_mask):
    valid = valid_mask.astype(jnp.float32)[:, None, :]
    low, vlow, z, inner, slab = exchange(count, images, valid)
    looks = look_coherences(z, inner, valid, low, vlow)
    return looks, slab


def solution(mesh):
    count = mesh.shape["pix"]
    in_specs = (P(("group", "pix"), None, None, None), P(("group", "pix"), None))
    out_specs = (P(("group", "pix"), None, None, None, None), P("group", None, None))
    return jax.shard_map(
        functools.partial(shards, count),
        mesh=mesh,
        in_specs=in_specs,
        out_specs=out_specs,
        check_vma=False,
    )
```

```python
import functools

import jax
import jax.numpy as jnp
from jax import lax
from jax.experimental import pallas as pl
from jax.experimental.pallas import tpu as pltpu
from jax.sharding import PartitionSpec as P

floor_power = 30.0
look_width = 21
lane = 128
below = 3
above = 2
width = 2 * lane
per_group = 5
MESH = pl.DeviceIdType.MESH
NT = (((1,), (1,)), ((), ()))


def group_start(g, cols):
    return min(g * per_group * look_width, cols - lane)


def put(z, v, acq, cols, r, image, weights):
    a, b = image[0], image[1]
    even = pl.ds(pl.multiple_of(r * width, lane), lane)
    odd = pl.ds(pl.multiple_of(r * width + lane, lane), lane)
    for n in range(z.shape[0]):
        s = group_start(n, cols)
        pa, pb = a[:, s : s + lane], b[:, s : s + lane]
        z[n, 0:acq, even] = pa
        z[n, 0:acq, odd] = pb
        z[n, lane : lane + acq, even] = -pb
        z[n, lane : lane + acq, odd] = pa
        w = weights[:, s : s + lane]
        v[n, :, even] = w
        v[n, :, odd] = w


def clear_padding(z, acq):
    @pl.loop(0, z.shape[0])
    def _(n):
        zeros = jnp.zeros((lane - acq, z.shape[2]), jnp.bfloat16)
        z[n, acq:lane, :] = zeros
        z[n, lane + acq : 2 * lane, :] = zeros


def masked_looks(lhs, x, weights, g, cols):
    first = g * per_group * look_width
    offset = first - jnp.minimum(first, cols - lane)
    lanes = jnp.bitwise_and(lax.broadcasted_iota(jnp.int32, weights.shape, 1), lane - 1)
    for n in range(per_group):
        lo = offset + n * look_width
        inside = (lanes >= lo) & (lanes < lo + look_width)
        chosen = jnp.where(inside, weights, 0.0).astype(jnp.bfloat16)
        lhs[n * lane : (n + 1) * lane, :] = x * chosen


def gram(lhs, first_row, last_row, right):
    k = pl.ds(first_row * width, (last_row - first_row + 1) * width)
    return lax.dot_general(lhs[:, k], right[:, k], NT, preferred_element_type=jnp.float32)


def finish(acc, acq, store):
    row_index = lax.broadcasted_iota(jnp.int32, (lane, lane), 0)
    col_index = lax.broadcasted_iota(jnp.int32, (lane, lane), 1)
    eye = row_index == col_index
    for n in range(per_group):
        at = pl.ds(n * lane, lane)
        real = acc[at, 0:lane]
        imag = acc[at, lane:width]
        diag = jnp.where(eye, real, 0.0)
        down = lax.rsqrt(jnp.maximum(jnp.sum(diag, axis=1, keepdims=True), floor_power))
        across = lax.rsqrt(jnp.maximum(jnp.sum(diag, axis=0, keepdims=True), floor_power))
        real = real * down * across
        imag = imag * down * across
        store(n, 0, real[0:acq, 0:acq].astype(jnp.bfloat16))
        store(n, 1, imag[0:acq, 0:acq].astype(jnp.bfloat16))


def exchange_kernel(
    count, rows, acq, cols,
    own_ref, valid_ref,
    low_ref, vlow_ref, z_hbm, inner_hbm, slab_ref,
    high_ref, vhigh_ref, z_high, v_high, lhs_high, acc_high,
    z, v, lhs, acc, inner, packed_ref, inbox, mine, result, full, gram_acc, zeros,
    halo_send, halo_recv, z_sem, inner_sem, zero_sem, send1, recv1, send2, recv2,
):
    me = lax.axis_index("pix")
    owners = packed_ref.shape[0]
    groups = z.shape[0]
    barrier = pltpu.get_barrier_semaphore()

    @pl.loop(1, count)
    def _(o):
        peer = lax.rem(me + o, count)
        pl.semaphore_signal(barrier, inc=1, device_id={"pix": peer}, device_id_type=MESH)

    pl.semaphore_wait(barrier, count - 1)

    def to_right(n):
        return halo(n, me + 1)

    def to_left(n):
        return halo(below + 1 + n, me - 1)

    def halo(n, peer):
        if n <= below:
            src, dst = (own_ref, low_ref) if n < below else (valid_ref, vlow_ref)
            at = pl.ds(rows - 1 - n, 1) if n < below else pl.ds(rows - below, below)
            to = pl.ds(below - 1 - n, 1) if n < below else pl.ds(0, below)
        else:
            m = n - below - 1
            src, dst = (own_ref, high_ref) if m < above else (valid_ref, vhigh_ref)
            at = to = pl.ds(m, 1) if m < above else pl.ds(0, above)
        return pltpu.make_async_remote_copy(
            src_ref=src.at[at], dst_ref=dst.at[to],
            send_sem=halo_send.at[n], recv_sem=halo_recv.at[n],
            device_id={"pix": peer}, device_id_type=MESH,
        )

    rights = (below,) + tuple(range(below))
    lefts = (above,) + tuple(range(above))

    def send(to_the_right, to_the_left):
        @pl.when(me < count - 1)
        def _():
            for n in to_the_right:
                to_right(n).start()

        @pl.when(me > 0)
        def _():
            for n in to_the_left:
                to_left(n).start()

    send(rights[:2], lefts[:2])

    def blank(dst, vdst, size):
        image = pltpu.make_async_copy(zeros.at[pl.ds(0, size)], dst, zero_sem)
        image.start()
        image.wait()
        vdst[...] = jnp.zeros_like(vdst)

    @pl.when(me == 0)
    def _():
        zeros[...] = jnp.zeros_like(zeros)
        blank(low_ref, vlow_ref, below)

    @pl.when(me == count - 1)
    def _():
        high_ref[...] = jnp.zeros_like(high_ref)
        vhigh_ref[...] = jnp.zeros_like(vhigh_ref)

    full[...] = jnp.zeros_like(full)
    gram_acc[...] = jnp.zeros_like(gram_acc)

    @pl.loop(0, rows)
    def _(r):
        image = own_ref[r]
        full[0:acq, :] = image[0]
        full[lane : lane + acq, :] = image[1]
        both = full[...]
        left = both * valid_ref[r].astype(jnp.bfloat16)
        gram_acc[...] += lax.dot_general(left, both, NT, preferred_element_type=jnp.float32)

    real = gram_acc[0:lane, 0:lane] + gram_acc[lane:, lane:]
    imag = gram_acc[lane:, 0:lane] - gram_acc[0:lane, lane:]
    row_index = lax.broadcasted_iota(jnp.int32, (lane, lane), 0)
    col_index = lax.broadcasted_iota(jnp.int32, (lane, lane), 1)
    packed = jnp.where(row_index >= col_index, real, imag)
    for n in range(owners):
        packed_ref[n] = packed[8 * n : 8 * n + 8, :]

    def remote(src, dst, send, recv, peer):
        return pltpu.make_async_remote_copy(
            src_ref=src, dst_ref=dst, send_sem=send, recv_sem=recv,
            device_id={"pix": peer}, device_id_type=MESH,
        )

    def scatter(peer):
        return remote(packed_ref.at[peer], inbox.at[me], send1.at[peer], recv1.at[me], peer)

    def arrived(peer):
        return remote(packed_ref.at[0], inbox.at[peer], send1.at[0], recv1.at[peer], peer)

    def spread(peer):
        return remote(mine, result.at[me], send2.at[peer], recv2.at[me], peer)

    def gathered(peer):
        return remote(mine, result.at[peer], send2.at[peer], recv2.at[peer], peer)

    @pl.loop(1, count)
    def _(o):
        peer = lax.rem(me + o, count)

        @pl.when(peer < owners)
        def _():
            scatter(peer).start()

    send(rights[2:3], lefts[2:])

    clear_padding(z, acq)

    @pl.loop(0, rows)
    def _(r):
        put(z, v, acq, cols, r, own_ref[r], valid_ref[r])

    z_copy = pltpu.make_async_copy(z, z_hbm, z_sem)
    z_copy.start()

    def inner_copy(look, g):
        at = pl.ds(g * per_group, per_group)
        return pltpu.make_async_copy(inner.at[look, at], inner_hbm.at[look, at], inner_sem.at[look, g])

    def inner_group(g):
        masked_looks(lhs, z[g, 0:lane, :], v[g], g, cols)
        acc[...] = gram(lhs, 1, rows - 1, z.at[g])

        def store(n, part, value):
            inner[0, g * per_group + n, part] = value

        finish(acc, acq, store)
        inner_copy(0, g).start()

    @pl.loop(0, groups)
    def _(g):
        inner_group(g)

    @pl.when(me < owners)
    def _():
        inbox[me] = packed_ref[me]

        @pl.loop(1, count)
        def _(o):
            arrived(lax.rem(me + o, count)).wait_recv()

        mine[...] = jnp.sum(inbox[...], axis=0)
        result[me] = mine[...]

        @pl.loop(1, count)
        def _(o):
            spread(lax.rem(me + o, count)).start()

    send(rights[3:], ())

    @pl.when(me < count - 1)
    def _():
        for n in lefts:
            to_left(n).wait_recv()

    clear_padding(z_high, acq)

    @pl.loop(0, above)
    def _(r):
        put(z_high, v_high, acq, cols, r, high_ref[r], vhigh_ref[r])

    @pl.loop(0, groups)
    def _(g):
        masked_looks(lhs, z[g, 0:lane, :], v[g], g, cols)
        masked_looks(lhs_high, z_high[g, 0:lane, :], v_high[g], g, cols)
        acc_high[...] = gram(lhs, rows - 5, rows - 1, z.at[g]) + gram(
            lhs_high, 0, above - 1, z_high.at[g]
        )

        def store(n, part, value):
            inner[1, g * per_group + n, part] = value

        finish(acc_high, acq, store)
        inner_copy(1, g).start()

    @pl.loop(1, count)
    def _(o):
        peer = lax.rem(me + o, count)

        @pl.when(peer < owners)
        def _():
            gathered(peer).wait_recv()

    packed = jnp.concatenate(
        [result[n] for n in range(owners)] + [jnp.zeros((lane - 8 * owners, lane), jnp.float32)],
        axis=0,
    )
    flipped = packed.T
    real = jnp.where(row_index >= col_index, packed, flipped)
    imag = jnp.where(row_index < col_index, packed, -flipped)
    imag = jnp.where(row_index == col_index, 0.0, imag)
    diag = jnp.where(row_index == col_index, packed, 0.0)
    scale = jnp.sqrt(jnp.sum(diag, axis=1, keepdims=True) * jnp.sum(diag, axis=0, keepdims=True))
    slab_ref[0] = (real / scale)[0:acq, 0:acq]
    slab_ref[1] = (imag / scale)[0:acq, 0:acq]

    z_copy.wait()

    @pl.loop(0, groups)
    def _(g):
        inner_copy(0, g).wait()
        inner_copy(1, g).wait()

    @pl.loop(1, count)
    def _(o):
        peer = lax.rem(me + o, count)

        @pl.when(peer < owners)
        def _():
            scatter(peer).wait_send()

        @pl.when(me < owners)
        def _():
            spread(peer).wait_send()

    @pl.when(me < count - 1)
    def _():
        for n in rights:
            to_right(n).wait_send()

    @pl.when(me > 0)
    def _():
        for n in lefts:
            to_left(n).wait_send()
        for n in rights:
            to_right(n).wait_recv()


def exchange(count, own, valid):
    rows, _, acq, cols = own.shape
    look_cols = cols // look_width
    groups = look_cols // per_group
    owners = pl.cdiv(acq, 8)
    vmem = pl.BlockSpec(memory_space=pltpu.VMEM)
    hbm = pl.BlockSpec(memory_space=pl.ANY)
    bf16, f32 = jnp.bfloat16, jnp.float32
    dma = pltpu.SemaphoreType.DMA
    return pl.pallas_call(
        functools.partial(exchange_kernel, count, rows, acq, cols),
        out_shape=(
            jax.ShapeDtypeStruct((below, 2, acq, cols), bf16),
            jax.ShapeDtypeStruct((below, 1, cols), f32),
            jax.ShapeDtypeStruct((groups, 2 * lane, rows * width), bf16),
            jax.ShapeDtypeStruct((2, look_cols, 2, acq, acq), bf16),
            jax.ShapeDtypeStruct((2, acq, acq), f32),
        ),
        in_specs=[vmem, vmem],
        out_specs=(hbm, vmem, hbm, hbm, vmem),
        scratch_shapes=[
            pltpu.VMEM((above, 2, acq, cols), bf16),
            pltpu.VMEM((above, 1, cols), f32),
            pltpu.VMEM((groups, 2 * lane, above * width), bf16),
            pltpu.VMEM((groups, 1, above * width), f32),
            pltpu.VMEM((per_group * lane, above * width), bf16),
            pltpu.VMEM((per_group * lane, width), f32),
            pltpu.VMEM((groups, 2 * lane, rows * width), bf16),
            pltpu.VMEM((groups, 1, rows * width), f32),
            pltpu.VMEM((per_group * lane, rows * width), bf16),
            pltpu.VMEM((per_group * lane, width), f32),
            pltpu.VMEM((2, look_cols, 2, acq, acq), bf16),
            pltpu.VMEM((owners, 8, lane), f32),
            pltpu.VMEM((count, 8, lane), f32),
            pltpu.VMEM((8, lane), f32),
            pltpu.VMEM((owners, 8, lane), f32),
            pltpu.VMEM((2 * lane, cols), bf16),
            pltpu.VMEM((2 * lane, 2 * lane), f32),
            pltpu.VMEM((below, 2, acq, cols), bf16),
            dma((below + above + 2,)), dma((below + above + 2,)), dma, dma((2, groups)), dma,
            dma((owners,)), dma((count,)), dma((count,)), dma((count,)),
        ],
        compiler_params=pltpu.CompilerParams(
            collective_id=0, has_side_effects=True, vmem_limit_bytes=48 << 20
        ),
        name="exchange",
    )(own, valid)


def looks_kernel(
    rows, acq, cols,
    z_ref, inner_ref, valid_ref, low_ref, vlow_ref,
    out_ref, z, v, v_own, lhs, lhs_halo, acc0, acc1,
):
    g = pl.program_id(0)
    @pl.when(g == 0)
    def _():
        clear_padding(z, acq)

        @pl.loop(0, below)
        def _(r):
            put(z, v, acq, cols, r, low_ref[r], vlow_ref[r])

        for r in range(rows):
            for n in range(v_own.shape[0]):
                s = group_start(n, cols)
                w = valid_ref[r][:, s : s + lane]
                v_own[n, :, pl.ds(r * width, lane)] = w
                v_own[n, :, pl.ds(r * width + lane, lane)] = w

    own, edge = z_ref.at[0], z.at[g]
    used = (rows // 2 + 2) * width
    masked_looks(lhs, z_ref[0, 0:lane, 0:used], v_own[g, :, 0:used], g, cols)
    masked_looks(lhs_halo, z[g, 0:lane, :], v[g], g, cols)

    def store(look):
        def put_out(n, part, value):
            out_ref[look, n, part] = value
        return put_out

    half = rows // 2
    common = gram(lhs, 0, half - 1, own)
    acc0[...] = common + gram(lhs_halo, 0, below - 1, edge)
    acc1[...] = common + (gram(lhs, half, half + 1, own) + gram(lhs_halo, below - 1, below - 1, edge))
    finish(acc0, acq, store(0))
    finish(acc1, acq, store(1))
    out_ref[2:4] = inner_ref[...]


def look_coherences(z, inner, valid, low, vlow):
    groups, _, wide = z.shape
    rows = wide // width
    _, look_cols, _, acq, _ = inner.shape
    cols = valid.shape[-1]
    whole = [valid, low, vlow]
    full = lambda shape: pl.BlockSpec(
        shape, lambda g: (0,) * len(shape), pipeline_mode=pl.Buffered(1)
    )
    return pl.pallas_call(
        functools.partial(looks_kernel, rows, acq, cols),
        grid=(groups,),
        out_shape=jax.ShapeDtypeStruct((rows // 2, look_cols, 2, acq, acq), jnp.bfloat16),
        in_specs=[
            pl.BlockSpec((1, 2 * lane, wide), lambda g: (g, 0, 0)),
            pl.BlockSpec((2, per_group, 2, acq, acq), lambda g: (0, g, 0, 0, 0)),
        ] + [full(x.shape) for x in whole],
        out_specs=pl.BlockSpec((rows // 2, per_group, 2, acq, acq), lambda g: (0, g, 0, 0, 0)),
        scratch_shapes=[
            pltpu.VMEM((groups, 2 * lane, below * width), jnp.bfloat16),
            pltpu.VMEM((groups, 1, below * width), jnp.float32),
            pltpu.VMEM((groups, 1, wide), jnp.float32),
            pltpu.VMEM((per_group * lane, (rows // 2 + 2) * width), jnp.bfloat16),
            pltpu.VMEM((per_group * lane, below * width), jnp.bfloat16),
        ] + [pltpu.VMEM((per_group * lane, width), jnp.float32)] * 2,
        compiler_params=pltpu.CompilerParams(vmem_limit_bytes=48 << 20),
        name="looks",
    )(z, inner, *whole)


def shards(count, images, valid_mask):
    valid = valid_mask.astype(jnp.float32)[:, None, :]
    low, vlow, z, inner, slab = exchange(count, images, valid)
    looks = look_coherences(z, inner, valid, low, vlow)
    return looks, slab


def solution(mesh):
    count = mesh.shape["pix"]
    in_specs = (P(("group", "pix"), None, None, None), P(("group", "pix"), None))
    out_specs = (P(("group", "pix"), None, None, None, None), P("group", None, None))
    return jax.shard_map(
        functools.partial(shards, count),
        mesh=mesh,
        in_specs=in_specs,
        out_specs=out_specs,
        check_vma=False,
    )
```
